128 devices in a mesh: section: 8 (over y, z_hi), dp: 16 (over z_lo, x, core).
Axes of the slice: x: 4, y: 4, z: 4 (z_hi: 2, z_lo: 2; z = z_hi * 2 + z_lo), core: 2. Of those that a mesh axis runs over, the one named last changes fastest.
Arguments:
- query_gradient_stack: float32 [8, 8192, 2048], P('section', 'dp'), may hold values from -6 to 6
- train_grads: float32 [8, 8192, 2048], P('section', 'dp'), may hold values from -6 to 6
- factor_slots: float32 [8, 16, 2048, 512], P('section', 'dp'), as said below
- owner: int32 [8, 4], P('section'), may hold values from 0 to 15, as said below
- train_count: int32 [16], P('dp'), may hold values from 128 to 512, as said below
Outputs:
- scores: float32 [16, 512, 1536], P('dp', 'section')
The draws below stay inside these ranges and needn't reach their ends.
Inputs may be any that keep to these rules, and one draw needn't show every extreme that they name: `owner`: for each layer the 4 entries are distinct data indices. `train_count`: some data index has all 512 training examples live. `factor_slots`: the diagonal entries of each factor lie between 0.9 and 2.1.
All inputs are finite; a program needn't handle non-finite values.
Results may differ from the reference program's by a relative error of at most 0.00019.
Values sent between devices are 32-bit elements; how exact they have to be, the bound alone decides.
A program may use at most 128 MiB of HBM per device.

```python
import math
import jax
import jax.numpy as jnp
from jax import lax

COORDS = 2048
PANEL = 512
PANELS = 4
ROWS = 512
LAYERS = 8
N_DP = 16


def panel_owners(key):
    layer_keys = jax.random.split(jax.random.fold_in(key, 7), LAYERS)
    return jax.vmap(lambda layer_key: jax.random.permutation(layer_key, N_DP)[:PANELS])(layer_keys).astype(jnp.int32)


def draw_owner(key, part):
    return panel_owners(key)


def draw_factor_slots(key, part):
    owner_list = panel_owners(key)
    noise_part = jax.random.normal(jax.random.fold_in(key, 11), (LAYERS, N_DP, COORDS, PANEL), jnp.float32) * (0.5 / math.sqrt(COORDS))
    diagonal = jax.random.uniform(jax.random.fold_in(key, 13), (LAYERS, COORDS), jnp.float32, 1.0, 2.0)
    block_keeper = (owner_list[:, :, None] == jnp.arange(N_DP)[None, None, :]).astype(jnp.float32)
    row_index = jnp.arange(COORDS)
    row_panel_lookup = (row_index[:, None] // PANEL == jnp.arange(PANELS)[None, :]).astype(jnp.float32)
    diagonal_flag = (row_index[:, None] % PANEL == jnp.arange(PANEL)[None, :]).astype(jnp.float32)
    row_in_slot = jnp.einsum('fda,od->fao', block_keeper, row_panel_lookup)
    boosted = row_in_slot * diagonal[:, None, :]
    return noise_part + boosted[:, :, :, None] * diagonal_flag[None, None, :, :]


def draw_train_count(key, part):
    counts = jax.random.randint(jax.random.fold_in(key, 17), (N_DP,), ROWS // 4, ROWS + 1)
    fullest = jax.random.randint(jax.random.fold_in(key, 19), (), 0, N_DP)
    return jnp.where(jnp.arange(N_DP) == fullest, ROWS, counts).astype(jnp.int32)


def steps_of(key, shape, cuts, low, top_value):
    level, own = 1.0, jax.random.fold_in(key, 6)
    for dim, parts in cuts:
        draws = jnp.exp(jax.random.uniform(jax.random.fold_in(own, dim), (parts,), jnp.float32, low / len(cuts), top_value / len(cuts)))
        level = level * jnp.repeat(draws, shape[dim] // parts).reshape([-1 if axis == dim else 1 for axis in range(len(shape))])
    return level


def scatter_about(stream_key, extent, deviation, limit, pieces=(), kind=jnp.bfloat16):
    entries = jax.random.normal(stream_key, extent, jnp.float32) * deviation
    if len(pieces) > 0:
        entries = steps_of(stream_key, extent, pieces, -0.22, 0.18) * entries
    return jnp.clip(entries, min=-limit, max=limit).astype(kind)


def setup_inputs(seed: int = 0) -> dict:
    key_of = jax.random.split(jax.random.key(seed), 6)
    return {
        "query_gradient_stack": scatter_about(key_of[0], (LAYERS, ROWS * N_DP, COORDS), 1.0, 6.0, ((0, 8), (1, 16)), jnp.float32),
        "train_grads": scatter_about(key_of[1], (LAYERS, ROWS * N_DP, COORDS), 1.0, 6.0, ((0, 8), (1, 16)), jnp.float32),
        "factor_slots": draw_factor_slots(jax.random.fold_in(key_of[5], 71), 0),
        "owner": draw_owner(jax.random.fold_in(key_of[5], 71), 0),
        "train_count": draw_train_count(jax.random.fold_in(key_of[5], 71), 0),
    }


def solve_layer(factor_full, gradient_rows):
    return lax.linalg.triangular_solve(factor_full, gradient_rows, left_side=False, lower=True, transpose_a=True)

def reference(query_gradient_stack, train_grads, factor_slots, owner, train_count):
    running = jnp.zeros((N_DP, ROWS, 3 * ROWS), jnp.float32)
    for layer_index in range(LAYERS):
        panel_set = factor_slots[layer_index][owner[layer_index]]
        factor_full = jnp.tril(jnp.transpose(panel_set, (1, 0, 2)).reshape(COORDS, COORDS))
        query_solved = solve_layer(factor_full, query_gradient_stack[layer_index]).reshape(N_DP, ROWS, COORDS)
        train_solved = solve_layer(factor_full, train_grads[layer_index]).reshape(N_DP, ROWS, COORDS)
        columns = jnp.concatenate([train_solved, jnp.roll(train_solved, 1, axis=0), jnp.roll(train_solved, 2, axis=0)], axis=1)
        running = running + jnp.einsum('dik,djk->dij', query_solved, columns, precision=lax.Precision.HIGHEST)
    counts = jnp.stack([train_count, jnp.roll(train_count, 1), jnp.roll(train_count, 2)], axis=1)
    valid = (jnp.arange(ROWS, dtype=jnp.int32)[None, None, :] < counts[:, :, None]).astype(jnp.float32)
    valid = valid.reshape(N_DP, 3 * ROWS)
    score_scale = (COORDS * LAYERS) ** (-0.5)
    return running * (score_scale * valid)[:, None, :]
```

```python
import jax
import jax.numpy as jnp
from jax import lax
from jax.experimental import pallas as pl
from jax.experimental.pallas import tpu as pltpu
from jax.sharding import PartitionSpec as P

COORDS = 2048
PANEL = 512
ROWS = 512
BLOCK = 256
SMALL = 128
BASE = 16
F32, BF16 = jnp.float32, jnp.bfloat16
NT = (((1,), (1,)), ((), ()))
NN = (((1,), (0,)), ((), ()))


def split(value):
    high = value.astype(BF16)
    return high, (value - high.astype(F32)).astype(BF16)


def dot3(a_high, a_low, b_high, b_low, dims=NT):
    def one(a, b):
        return lax.dot_general(a, b, dims, preferred_element_type=F32)

    return one(a_high, b_high) + (one(a_high, b_low) + one(a_low, b_high))


def dot_f32(a, b):
    return lax.dot_general(
        a, b, NN, precision=lax.Precision.HIGHEST, preferred_element_type=F32
    )


def invert_small(block):
    row = lax.broadcasted_iota(jnp.int32, (SMALL, SMALL), 0)
    col = lax.broadcasted_iota(jnp.int32, (SMALL, SMALL), 1)
    block = jnp.where(row >= col, block, 0.0)
    diagonal = jnp.sum(jnp.where(row == col, block, 0.0), axis=1, keepdims=True)
    scale = (1.0 / diagonal).reshape(SMALL // BASE, BASE, 1)
    inner = jnp.where(row // BASE == col // BASE, block, 0.0)
    inverse = jnp.where(row == col, 1.0, 0.0).reshape(SMALL // BASE, BASE, SMALL)
    place = lax.broadcasted_iota(jnp.int32, inverse.shape, 1)
    for step in range(BASE):
        factor = jnp.sum(jnp.where(col % BASE == step, inner, 0.0), axis=1, keepdims=True)
        factor = factor.reshape(SMALL // BASE, BASE, 1)
        pivot = inverse[:, step : step + 1, :] * scale[:, step : step + 1, :]
        below = inverse - jnp.where(place > step, factor, 0.0) * pivot
        inverse = jnp.where(place == step, pivot, below)
    inverse = inverse.reshape(SMALL, SMALL)
    size = BASE
    while size < SMALL:
        left = (row // size) % 2 == 1
        pick = left & (col // size == row // size - 1)
        inner = dot_f32(jnp.where(pick, block, 0.0), inverse)
        inverse = inverse - dot_f32(inverse, inner)
        size *= 2
    return inverse


def solve_kernel(
    q_hbm, t_hbm, p0, p1, p2, p3, count_ref, x_ref,
    l_high, l_low, x_high, x_low, w_high, w_low, diag, copy_sem,
):
    panels = (p0, p1, p2, p3)
    copies = [
        pltpu.make_async_copy(source, x_ref.at[index], copy_sem.at[index])
        for index, source in enumerate((q_hbm, t_hbm))
    ]
    for copy in copies:
        copy.start()
    for number, panel in enumerate(panels):
        first = number * PANEL
        for part in range(PANEL // SMALL):
            at = part * SMALL
            diag[number * (PANEL // SMALL) + part] = panel[at : at + SMALL, at : at + SMALL]

        @pl.loop(0, (COORDS - first) // BLOCK)
        def _(step):
            rows = pl.ds(pl.multiple_of(step * BLOCK, BLOCK), BLOCK)
            there = pl.ds(pl.multiple_of(first + step * BLOCK, BLOCK), BLOCK)
            high, low = split(panel[rows, :])
            l_high[there, first : first + PANEL] = high
            l_low[there, first : first + PANEL] = low

    @pl.loop(0, COORDS // SMALL // 4)
    def _(step):
        for index in range(4):
            diag[step * 4 + index] = invert_small(diag[step * 4 + index])

    w_high[...] = jnp.zeros_like(w_high)
    w_low[...] = jnp.zeros_like(w_low)
    for block in range(COORDS // BLOCK):
        panel, at = panels[block // 2], (block % 2) * BLOCK
        upper, lower = diag[2 * block], diag[2 * block + 1]
        cross = panel[at + SMALL : at + BLOCK, at : at + SMALL]
        corner = -dot_f32(lower, dot_f32(cross, upper))
        base = block * BLOCK
        for value, rows, cols in ((upper, 0, 0), (corner, SMALL, 0), (lower, SMALL, SMALL)):
            high, low = split(value)
            w_high[base + rows : base + rows + SMALL, cols : cols + SMALL] = high
            w_low[base + rows : base + rows + SMALL, cols : cols + SMALL] = low

    for copy in copies:
        copy.wait()
    for block in range(COORDS // BLOCK):
        base = block * BLOCK
        cols = slice(base, base + BLOCK)

        @pl.loop(0, 2)
        def _(half):
            pending = x_ref[half, :, cols]
            if block:
                pending = pending - dot3(
                    x_high[half, :, :base], x_low[half, :, :base], l_high[cols, :base], l_low[cols, :base]
                )
            high, low = split(pending)
            solved = dot3(high, low, w_high[cols, :], w_low[cols, :])
            x_ref[half, :, cols] = solved
            high, low = split(solved)
            x_high[half, :, cols] = high
            x_low[half, :, cols] = low

    place = lax.broadcasted_iota(jnp.int32, (ROWS, SMALL), 0)
    keep = jnp.where(place < count_ref[0], F32(1.0 / 128.0), F32(0.0))
    for part in range(COORDS // SMALL):
        cols = slice(part * SMALL, (part + 1) * SMALL)
        x_ref[1, :, cols] = x_ref[1, :, cols] * keep


def solve(query, train, panels, count):
    vmem, anyspace = pl.BlockSpec(memory_space=pltpu.VMEM), pl.BlockSpec(memory_space=pl.ANY)
    return pl.pallas_call(
        solve_kernel,
        out_shape=jax.ShapeDtypeStruct((2, ROWS, COORDS), F32),
        in_specs=[anyspace] * 2 + [vmem] * 4 + [pl.BlockSpec(memory_space=pltpu.SMEM)],
        out_specs=vmem,
        scratch_shapes=[
            pltpu.VMEM((COORDS, COORDS), BF16),
            pltpu.VMEM((COORDS, COORDS), BF16),
            pltpu.VMEM((2, ROWS, COORDS), BF16),
            pltpu.VMEM((2, ROWS, COORDS), BF16),
            pltpu.VMEM((COORDS, BLOCK), BF16),
            pltpu.VMEM((COORDS, BLOCK), BF16),
            pltpu.VMEM((COORDS // SMALL, SMALL, SMALL), F32),
            pltpu.SemaphoreType.DMA((2,)),
        ],
        compiler_params=pltpu.CompilerParams(vmem_limit_bytes=60 << 20),
        name="solve",
    )(query, train, *panels, count)


def spread(block, axis, source):
    block = jnp.where(lax.axis_index(axis) == source, block, jnp.zeros_like(block))
    return lax.psum(block, axis)


def score(left, right):
    return lax.dot_general(
        left, right, NT, precision=lax.Precision.HIGH, preferred_element_type=F32
    )


def body(query_gradient_stack, train_grads, factor_slots, owner, train_count):
    count = lax.axis_size("dp")
    me = lax.axis_index("dp")
    even = me % 2 == 0
    slot, owners = factor_slots[0, 0], owner[0]
    panels = [spread(slot[j * PANEL :], "dp", owners[j]) for j in range(COORDS // PANEL)]
    solved = solve(query_gradient_stack[0], train_grads[0], panels, train_count)
    query, train = solved[0], solved[1]
    evens = range(0, count, 2)
    before = lax.ppermute(train, "dp", [(d, (d + 1) % count) for d in range(count)])
    later_query = lax.ppermute(query, "dp", [((d + 2) % count, d) for d in evens])
    before_that = lax.ppermute(before, "dp", [(d, d + 1) for d in evens])
    first = score(query, train)
    second = score(query, before)
    third = score(jnp.where(even, later_query, query), jnp.where(even, train, before_that))
    tiles = jnp.concatenate([first, second, third], axis=1)
    summed = lax.psum_scatter(tiles, "section", scatter_dimension=0, tiled=True)
    last = summed[:, 2 * ROWS :]
    moved = lax.ppermute(last, "dp", [(d, (d + 2) % count) for d in evens])
    return jnp.concatenate([summed[:, : 2 * ROWS], jnp.where(even, moved, last)], axis=1)[None]


def solution(mesh):
    in_specs = (
        P("section", "dp", None),
        P("section", "dp", None),
        P("section", "dp", None, None),
        P("section", None),
        P("dp"),
    )
    out_specs = P("dp", "section", None)
    return jax.shard_map(body, mesh=mesh, in_specs=in_specs, out_specs=out_specs, check_vma=False)
```

```python
import jax
import jax.numpy as jnp
from jax import lax
from jax.experimental import pallas as pl
from jax.experimental.pallas import tpu as pltpu
from jax.sharding import PartitionSpec as P

COORDS = 2048
PANEL = 512
ROWS = 512
BLOCK = 256
SMALL = 128
BASE = 16
F32, BF16 = jnp.float32, jnp.bfloat16
NT = (((1,), (1,)), ((), ()))
NN = (((1,), (0,)), ((), ()))
MESH = pl.DeviceIdType.MESH
PANELS = COORDS // PANEL
CHUNK = 128
PART = 16


def split(value):
    high = value.astype(BF16)
    return high, (value - high.astype(F32)).astype(BF16)


def dot3(a_high, a_low, b_high, b_low, dims=NT):
    def one(a, b):
        return lax.dot_general(a, b, dims, preferred_element_type=F32)

    return one(a_high, b_high) + (one(a_high, b_low) + one(a_low, b_high))


def dot_f32(a, b):
    return lax.dot_general(
        a, b, NN, precision=lax.Precision.HIGHEST, preferred_element_type=F32
    )


def invert_small(block):
    row = lax.broadcasted_iota(jnp.int32, (SMALL, SMALL), 0)
    col = lax.broadcasted_iota(jnp.int32, (SMALL, SMALL), 1)
    block = jnp.where(row >= col, block, 0.0)
    diagonal = jnp.sum(jnp.where(row == col, block, 0.0), axis=1, keepdims=True)
    scale = (1.0 / diagonal).reshape(SMALL // BASE, BASE, 1)
    inner = jnp.where(row // BASE == col // BASE, block, 0.0)
    inverse = jnp.where(row == col, 1.0, 0.0).reshape(SMALL // BASE, BASE, SMALL)
    place = lax.broadcasted_iota(jnp.int32, inverse.shape, 1)
    for step in range(BASE):
        factor = jnp.sum(jnp.where(col % BASE == step, inner, 0.0), axis=1, keepdims=True)
        factor = factor.reshape(SMALL // BASE, BASE, 1)
        pivot = inverse[:, step : step + 1, :] * scale[:, step : step + 1, :]
        below = inverse - jnp.where(place > step, factor, 0.0) * pivot
        inverse = jnp.where(place == step, pivot, below)
    inverse = inverse.reshape(SMALL, SMALL)
    size = BASE
    while size < SMALL:
        left = (row // size) % 2 == 1
        pick = left & (col // size == row // size - 1)
        inner = dot_f32(jnp.where(pick, block, 0.0), inverse)
        inverse = inverse - dot_f32(inverse, inner)
        size *= 2
    return inverse


def load_factor(panels, stage, stage_sem, l_high, l_low, diag, cross):
    pieces = [(group, number) for group in range(PANELS) for number in range(group + 1)]

    def fetch(index):
        group, number = pieces[index]
        rows = pl.ds((group - number) * PANEL, PANEL)
        slot = index % 2
        return pltpu.make_async_copy(panels[number].at[rows, :], stage.at[slot], stage_sem.at[slot])

    fetch(0).start()
    for index, (group, number) in enumerate(pieces):
        if index + 1 < len(pieces):
            fetch(index + 1).start()
        fetch(index).wait()
        slot = index % 2
        cols = slice(number * PANEL, (number + 1) * PANEL)

        @pl.loop(0, PANEL // CHUNK)
        def _(step):
            high, low = split(stage[slot, pl.ds(pl.multiple_of(step * CHUNK, CHUNK), CHUNK), :])
            there = pl.ds(pl.multiple_of(group * PANEL + step * CHUNK, CHUNK), CHUNK)
            l_high[there, cols] = high
            l_low[there, cols] = low

        if group == number:
            for part in range(PANEL // SMALL):
                at = slice(part * SMALL, (part + 1) * SMALL)
                diag[group * (PANEL // SMALL) + part] = stage[slot, at, at]
            for part in range(PANEL // BLOCK):
                at = part * BLOCK
                cross[group * (PANEL // BLOCK) + part] = stage[
                    slot, at + SMALL : at + BLOCK, at : at + SMALL
                ]


def invert_blocks(diag, cross, w_high, w_low):
    @pl.loop(0, COORDS // SMALL // 4)
    def _(step):
        for index in range(4):
            diag[step * 4 + index] = invert_small(diag[step * 4 + index])

    w_high[...] = jnp.zeros_like(w_high)
    w_low[...] = jnp.zeros_like(w_low)

    @pl.loop(0, COORDS // BLOCK // 2)
    def _(step):
        for index in range(2):
            block = step * 2 + index
            upper, lower = diag[2 * block], diag[2 * block + 1]
            corner = -dot_f32(lower, dot_f32(cross[block], upper))
            for value, rows, cols in ((upper, 0, 0), (corner, SMALL, 0), (lower, SMALL, SMALL)):
                high, low = split(value)
                there = pl.ds(pl.multiple_of(block * BLOCK + rows, SMALL), SMALL)
                w_high[there, cols : cols + SMALL] = high
                w_low[there, cols : cols + SMALL] = low


def solve_half(half, x_ref, x_high, x_low, l_high, l_low, w_high, w_low):
    for block in range(COORDS // BLOCK):
        base = block * BLOCK
        cols = slice(base, base + BLOCK)
        pending = x_ref[half, :, cols]
        if block:
            pending = pending - dot3(
                x_high[half, :, :base], x_low[half, :, :base], l_high[cols, :base], l_low[cols, :base]
            )
        high, low = split(pending)
        solved = dot3(high, low, w_high[cols, :], w_low[cols, :])
        x_ref[half, :, cols] = solved
        high, low = split(solved)
        x_high[half, :, cols] = high
        x_low[half, :, cols] = low


def score_kernel(
    q_hbm, t_hbm, p0, p1, p2, p3, count_ref, out_ref,
    l_high, l_low, x_ref, x_high, x_low, w_high, w_low, diag, cross, stage,
    a_in, b_in, c_high, c_low, tiles, first_in, second_out, second_in, kept, third_out, third_in,
    load_sem, stage_sem, a_send, a_recv, b_send, b_recv, r_send,
    f_send, f_recv, s_send, s_recv, m_send, m_recv,
):
    me, section = lax.axis_index("dp"), lax.axis_index("section")
    count = lax.axis_size("dp")
    rings, row_of, half_of = 4, section // 2, section % 2
    even = me % 2 == 0
    odd = me % 2 == 1
    after, before = lax.rem(me + 1, count), lax.rem(me + count - 1, count)
    after_two, before_two = lax.rem(me + 2, count), lax.rem(me + count - 2, count)

    def section_at(steps):
        return lax.rem(row_of + steps, rings) * 2 + half_of

    partner = row_of * 2 + 1 - half_of
    barrier = pltpu.get_barrier_semaphore()
    for other in (after, before, after_two, before_two):
        pl.semaphore_signal(barrier, inc=1, device_id={"dp": other}, device_id_type=MESH)
    for other in (section_at(1), section_at(2), section_at(3), partner):
        pl.semaphore_signal(barrier, inc=1, device_id={"section": other}, device_id_type=MESH)

    copies = [
        pltpu.make_async_copy(source, x_ref.at[index], load_sem.at[index])
        for index, source in enumerate((q_hbm, t_hbm))
    ]
    for copy in copies:
        copy.start()
    load_factor((p0, p1, p2, p3), stage, stage_sem, l_high, l_low, diag, cross)
    for copy in copies:
        copy.wait()
    place = lax.broadcasted_iota(jnp.int32, (ROWS, SMALL), 0)
    keep = jnp.where(place < count_ref[0], F32(1.0 / 128.0), F32(0.0))
    for part in range(COORDS // SMALL):
        cols = slice(part * SMALL, (part + 1) * SMALL)
        x_ref[1, :, cols] = x_ref[1, :, cols] * keep
    invert_blocks(diag, cross, w_high, w_low)
    pl.semaphore_wait(barrier, 8)

    def remote(source, target, send, recv, where):
        return pltpu.make_async_remote_copy(
            src_ref=source, dst_ref=target, send_sem=send, recv_sem=recv,
            device_id=where, device_id_type=MESH,
        )

    def send_train(part):
        rows = pl.ds(pl.multiple_of(part * CHUNK, CHUNK), CHUNK)
        return remote(x_ref.at[1, rows, :], a_in.at[part], a_send.at[part], a_recv.at[part], {"dp": after})

    def send_query(part, piece):
        rows = pl.ds(pl.multiple_of(piece * 64 + part * PART, PART), PART)
        there = pl.ds(piece * PART, PART)
        return remote(
            x_ref.at[0, rows, :], b_in.at[part, there, :], b_send.at[part], b_recv.at[part], {"dp": before_two}
        )

    def relay(part):
        return remote(a_in.at[part], b_in.at[part], r_send.at[part], b_recv.at[part], {"dp": after})

    @pl.loop(0, 2)
    def _(step):
        half = lax.rem(step + me, 2)
        solve_half(half, x_ref, x_high, x_low, l_high, l_low, w_high, w_low)

        @pl.when(half == 1)
        def _():
            for part in range(4):
                send_train(part).start()

        @pl.when((half == 0) & even)
        def _():
            for part in range(4):
                for piece in range(8):
                    send_query(part, piece).start()

    def chunk(part):
        return pl.ds(pl.multiple_of(part * CHUNK, CHUNK), CHUNK)

    def small_rows(part, base):
        return pl.ds(pl.multiple_of(base + part * PART, PART), PART)

    def first_column(tile, part, steps):
        to = lax.rem(row_of + steps, rings)
        rows = pl.ds(pl.multiple_of(to * 128, 128), 128)
        at = tile * 4 + part
        return remote(
            tiles.at[tile, rows, chunk(part)], first_in.at[tile, steps - 1, :, chunk(part)],
            f_send.at[at, steps - 1], f_recv.at[at, steps - 1], {"section": section_at(steps)},
        )

    def first_row(part, steps, side):
        to = lax.rem(row_of + steps, rings)
        at = 8 + part
        return remote(
            tiles.at[2, small_rows(part, to * 128 + side * 64), :],
            first_in.at[2, steps - 1, small_rows(part, side * 64), :],
            f_send.at[at, steps - 1], f_recv.at[at, steps - 1], {"section": section_at(steps)},
        )

    def column_piece(tile, part, high, low):
        tiles[tile, :, chunk(part)] = dot3(x_high[0], x_low[0], high, low)
        for steps in (1, 2, 3):
            first_column(tile, part, steps).start()

    def first_waits(tile, part):
        for steps in (1, 2, 3):
            first_column(tile, part, steps).wait()

    def sum_columns(tile, part):
        first_waits(tile, part)
        for mine in (True, False):
            side = half_of if mine else 1 - half_of
            there = pl.ds(pl.multiple_of(side * 64, 64), 64)
            rows = pl.ds(pl.multiple_of(row_of * 128 + side * 64, 64), 64)
            total = tiles[tile, rows, chunk(part)]
            for steps in range(3):
                total = total + first_in[tile, steps, there, chunk(part)]
            if mine:
                kept[tile, :, chunk(part)] = total
            else:
                second_out[tile, :, chunk(part)] = total
        second_column(tile, part).start()

    def second_column(tile, part):
        at = tile * 4 + part
        return remote(
            second_out.at[tile, :, chunk(part)], second_in.at[tile, :, chunk(part)],
            s_send.at[at], s_recv.at[at], {"section": partner},
        )

    def end_columns(tile, part):
        second_column(tile, part).wait()
        there = pl.ds(pl.multiple_of(tile * ROWS + part * CHUNK, CHUNK), CHUNK)
        out_ref[:, there] = kept[tile, :, chunk(part)] + second_in[tile, :, chunk(part)]

    def sum_rows(part):
        first_waits(2, part)
        for mine in (True, False):
            side = half_of if mine else 1 - half_of
            total = tiles[2, small_rows(part, row_of * 128 + side * 64), :]
            for steps in range(3):
                total = total + first_in[2, steps, small_rows(part, side * 64), :]
            if mine:
                kept[2, small_rows(part, 0), :] = total
            else:
                second_out[2, small_rows(part, 0), :] = total
        second_row(part).start()

    def second_row(part):
        at = 8 + part
        return remote(
            second_out.at[2, small_rows(part, 0), :], second_in.at[2, small_rows(part, 0), :],
            s_send.at[at], s_recv.at[at], {"section": partner},
        )

    def move(part):
        return remote(
            third_out.at[small_rows(part, 0), :], third_in.at[small_rows(part, 0), :],
            m_send.at[part], m_recv.at[part], {"dp": after_two},
        )

    def end_rows(part):
        second_row(part).wait()
        rows = small_rows(part, 0)
        third_out[rows, :] = kept[2, rows, :] + second_in[2, rows, :]
        move(part).start()

    @pl.loop(0, 4)
    def _(part):
        column_piece(0, part, x_high[1, chunk(part), :], x_low[1, chunk(part), :])

    @pl.loop(0, 7)
    def _(step):
        @pl.when(step < 4)
        def _():
            send_train(step).wait()

            @pl.when(even)
            def _():
                relay(step).start()

            c_high[...], c_low[...] = split(a_in[step])
            column_piece(1, step, c_high[...], c_low[...])
            pltpu.make_async_copy(b_in.at[step], b_in.at[step], b_recv.at[step]).wait()
            c_high[...], c_low[...] = split(b_in[step])

            @pl.when(odd)
            def _():
                column_piece(2, step, c_high[...], c_low[...])

            @pl.when(even)
            def _():
                made = dot3(c_high[...], c_low[...], x_high[1], x_low[1])
                for piece in range(8):
                    tiles[2, small_rows(step, piece * 64), :] = made[piece * PART : (piece + 1) * PART]
                for steps in (1, 2, 3):
                    for side in range(2):
                        first_row(step, steps, side).start()

            sum_columns(0, step)

        @pl.when((step >= 1) & (step < 5))
        def _():
            sum_columns(1, step - 1)

            @pl.when(odd)
            def _():
                sum_columns(2, step - 1)

            @pl.when(even)
            def _():
                sum_rows(step - 1)

            end_columns(0, step - 1)

        @pl.when((step >= 2) & (step < 6))
        def _():
            end_columns(1, step - 2)

            @pl.when(odd)
            def _():
                end_columns(2, step - 2)

            @pl.when(even)
            def _():
                end_rows(step - 2)

        @pl.when((step >= 3) & even)
        def _():
            move(step - 3).wait()
            out_ref[small_rows(step - 3, 0), 2 * ROWS :] = third_in[small_rows(step - 3, 0), :]

    @pl.when(even)
    def _():
        for part in range(4):
            relay(part).wait_send()
            pltpu.make_async_copy(b_in.at[part], b_in.at[part], b_send.at[part]).wait()


def scores_of(query, train, panels, count):
    vmem, anyspace = pl.BlockSpec(memory_space=pltpu.VMEM), pl.BlockSpec(memory_space=pl.ANY)
    dma = pltpu.SemaphoreType.DMA
    return pl.pallas_call(
        score_kernel,
        out_shape=jax.ShapeDtypeStruct((64, 3 * ROWS), F32),
        in_specs=[anyspace] * 6 + [pl.BlockSpec(memory_space=pltpu.SMEM)],
        out_specs=vmem,
        scratch_shapes=[
            pltpu.VMEM((COORDS, COORDS), BF16),
            pltpu.VMEM((COORDS, COORDS), BF16),
            pltpu.VMEM((2, ROWS, COORDS), F32),
            pltpu.VMEM((2, ROWS, COORDS), BF16),
            pltpu.VMEM((2, ROWS, COORDS), BF16),
            pltpu.VMEM((COORDS, BLOCK), BF16),
            pltpu.VMEM((COORDS, BLOCK), BF16),
            pltpu.VMEM((COORDS // SMALL, SMALL, SMALL), F32),
            pltpu.VMEM((COORDS // BLOCK, SMALL, SMALL), F32),
            pltpu.VMEM((2, PANEL, PANEL), F32),
            pltpu.VMEM((4, CHUNK, COORDS), F32),
            pltpu.VMEM((4, CHUNK, COORDS), F32),
            pltpu.VMEM((CHUNK, COORDS), BF16),
            pltpu.VMEM((CHUNK, COORDS), BF16),
            pltpu.VMEM((3, ROWS, ROWS), F32),
            pltpu.VMEM((3, 3, 128, ROWS), F32),
            pltpu.VMEM((3, 64, ROWS), F32),
            pltpu.VMEM((3, 64, ROWS), F32),
            pltpu.VMEM((3, 64, ROWS), F32),
            pltpu.VMEM((64, ROWS), F32),
            pltpu.VMEM((64, ROWS), F32),
            dma((2,)), dma((2,)), dma((4,)), dma((4,)), dma((4,)), dma((4,)), dma((4,)),
            dma((12, 3)), dma((12, 3)), dma((12,)), dma((12,)), dma((4,)), dma((4,)),
        ],
        compiler_params=pltpu.CompilerParams(
            vmem_limit_bytes=63 << 20, collective_id=0, has_side_effects=True
        ),
        name="scores",
    )(query, train, *panels, count)


def spread(block, axis, source):
    block = jnp.where(lax.axis_index(axis) == source, block, jnp.zeros_like(block))
    return lax.psum(block, axis)


def body(query_gradient_stack, train_grads, factor_slots, owner, train_count):
    slot, owners = factor_slots[0, 0], owner[0]
    panels = [spread(slot[j * PANEL :], "dp", owners[j]) for j in range(PANELS)]
    return scores_of(query_gradient_stack[0], train_grads[0], panels, train_count)[None]


def solution(mesh):
    in_specs = (
        P("section", "dp", None),
        P("section", "dp", None),
        P("section", "dp", None, None),
        P("section", None),
        P("dp"),
    )
    out_specs = P("dp", "section", None)
    return jax.shard_map(body, mesh=mesh, in_specs=in_specs, out_specs=out_specs, check_vma=False)
```

```python
import jax
import jax.numpy as jnp
from jax import lax
from jax.experimental import pallas as pl
from jax.experimental.pallas import tpu as pltpu
from jax.sharding import PartitionSpec as P

COORDS = 2048
PANEL = 512
ROWS = 512
BLOCK = 256
SMALL = 128
BASE = 16
F32, BF16 = jnp.float32, jnp.bfloat16
NT = (((1,), (1,)), ((), ()))
NN = (((1,), (0,)), ((), ()))
MESH = pl.DeviceIdType.MESH
PANELS = COORDS // PANEL
CHUNK = 128
PART = 16
PEERS = 16
STRIP = PANEL // PEERS
Z_ROWS = STRIP // 2
PIECES = [group * (group + 1) // 2 for group in range(PANELS + 1)]


def split(value):
    high = value.astype(BF16)
    return high, (value - high.astype(F32)).astype(BF16)


def dot3(a_high, a_low, b_high, b_low, dims=NT):
    def one(a, b):
        return lax.dot_general(a, b, dims, preferred_element_type=F32)

    return one(a_high, b_high) + (one(a_high, b_low) + one(a_low, b_high))


def invert_small(blocks):
    row = lax.broadcasted_iota(jnp.int32, (SMALL, SMALL), 0)
    col = lax.broadcasted_iota(jnp.int32, (SMALL, SMALL), 1)
    groups = (SMALL // BASE, BASE)

    def substituted(block):
        diagonal = jnp.sum(jnp.where(row == col, block, 0.0), axis=1, keepdims=True)
        scale = (1.0 / diagonal).reshape(*groups, 1)
        inner = jnp.where(row // BASE == col // BASE, block, 0.0)
        inverse = jnp.where(row == col, 1.0, 0.0).reshape(*groups, SMALL)
        place = lax.broadcasted_iota(jnp.int32, inverse.shape, 1)
        for step in range(BASE):
            factor = jnp.sum(jnp.where(col % BASE == step, inner, 0.0), axis=1, keepdims=True)
            factor = jnp.where(place > step, factor.reshape(*groups, 1), 0.0)
            pivot = inverse[:, step : step + 1, :] * scale[:, step : step + 1, :]
            inverse = jnp.where(place == step, pivot, inverse - factor * pivot)
        return inverse.reshape(SMALL, SMALL)

    inverses = [substituted(block) for block in blocks]
    size = BASE
    while size < SMALL:
        pick = ((row // size) % 2 == 1) & (col // size == row // size - 1)
        halves = [split(inverse) for inverse in inverses]
        inner = [
            split(dot3(*split(jnp.where(pick, block, 0.0)), high, low, NN))
            for block, (high, low) in zip(blocks, halves)
        ]
        inverses = [
            inverse - dot3(*half, *middle, NN)
            for inverse, half, middle in zip(inverses, halves, inner)
        ]
        size *= 2
    return inverses


def load_group(group, factor, stage, stage_sem, l_high, l_low, w_high, w_low):
    def fetch(number):
        slot = number % 2
        return pltpu.make_async_copy(factor.at[PIECES[group] + number], stage.at[slot], stage_sem.at[slot])

    def strips(slot, first, rows, cols):
        part = stage[slot, first // STRIP : (first + rows) // STRIP, :, cols]
        return part.reshape(rows, part.shape[-1])

    fetch(0).start()
    for number in range(group + 1):
        if number < group:
            fetch(number + 1).start()
        fetch(number).wait()
        cols = slice(number * PANEL, (number + 1) * PANEL)

        @pl.loop(0, PANEL // CHUNK)
        def _(step):
            part = stage[number % 2, pl.ds(step * (CHUNK // STRIP), CHUNK // STRIP)]
            high, low = split(part.reshape(CHUNK, PANEL))
            there = pl.ds(pl.multiple_of(group * PANEL + step * CHUNK, CHUNK), CHUNK)
            l_high[there, cols] = high
            l_low[there, cols] = low

    slot = group % 2
    inverses = invert_small(
        [strips(slot, at, SMALL, slice(at, at + SMALL)) for at in range(0, PANEL, SMALL)]
    )
    for part in range(PANEL // BLOCK):
        at = part * BLOCK
        upper, lower = inverses[2 * part], inverses[2 * part + 1]
        cross = strips(slot, at + SMALL, SMALL, slice(at, at + SMALL))
        corner = -dot3(*split(lower), *split(dot3(*split(cross), *split(upper), NN)), NN)
        base = group * PANEL + at
        blank = jnp.zeros((SMALL, SMALL), F32)
        for value, rows, cols in ((upper, 0, 0), (corner, SMALL, 0), (lower, SMALL, SMALL), (blank, 0, SMALL)):
            high, low = split(value)
            w_high[base + rows : base + rows + SMALL, cols : cols + SMALL] = high
            w_low[base + rows : base + rows + SMALL, cols : cols + SMALL] = low


def solve_group(group, half, x_ref, x_high, x_low, l_high, l_low, w_high, w_low):
    base = group * PANEL
    cols = slice(base, base + PANEL)
    pending = x_ref[half, :, cols]
    if group:
        pending = pending - dot3(
            x_high[half, :, :base], x_low[half, :, :base], l_high[cols, :base], l_low[cols, :base]
        )
    for number in range(PANEL // BLOCK):
        at = base + number * BLOCK
        here, known = slice(at, at + BLOCK), slice(base, at)
        part = pending[:, number * BLOCK : (number + 1) * BLOCK]
        if number:
            part = part - dot3(
                x_high[half, :, known], x_low[half, :, known], l_high[here, known], l_low[here, known]
            )
        high, low = split(part)
        solved = dot3(high, low, w_high[here, :], w_low[here, :])
        x_ref[half, :, here] = solved
        high, low = split(solved)
        x_high[half, :, here] = high
        x_low[half, :, here] = low


def device_at(z, x, core):
    return lax.rem(z, 2) * 8 + lax.rem(x, 4) * 2 + lax.rem(core, 2)


ROLES = (
    "z", "left", "right", "far_lo", "far_hi", "z_left_z", "z_right_z", "z_left_x", "z_right_x",
    "z_far_lo", "z_far_hi", "z_far_x",
) + tuple("core%d" % number for number in range(8))
SENDS = 24
ALL, Z_PART, X_PART = (0, STRIP), (0, Z_ROWS), (Z_ROWS, STRIP - Z_ROWS)
FULL, LOW, HIGH = (0, PANEL), (0, PANEL // 2), (PANEL // 2, PANEL // 2)


class Exchange:
    def __init__(self, slot, owner, factor, gathered, mine, sems):
        self.slot, self.owner, self.factor, self.gathered, self.mine = slot, owner, factor, gathered, mine
        self.spread_send, self.spread_recv, self.local, self.pass_send, self.pass_recv = sems
        me = self.me = lax.axis_index("dp")
        self.z, self.x, self.core = z, x, core = me // 8, (me // 2) % 4, me % 2
        order = ((1, 0), (0, 1), (1, 3), (0, 2), (1, 1), (0, 3), (1, 2), (0, 0))
        self.peers = [
            device_at(z + dz, x + dx, core + dc) for dz, dx in order for dc in (0, 1) if dz or dx or dc
        ]
        self.z_peer, self.other = device_at(z + 1, x, core), device_at(z, x, core + 1)
        self.right, self.left = device_at(z, x + 1, core), device_at(z, x + 3, core)
        self.far = device_at(z, x + 2, core)
        self.z_left, self.z_right = device_at(z + 1, x + 3, core), device_at(z + 1, x + 1, core)
        self.z_far = device_at(z + 1, x + 2, core)
        self.started = [[] for _ in range(PANELS)]

    def remote(self, source, target, send, recv, where):
        return pltpu.make_async_remote_copy(
            src_ref=source, dst_ref=target, send_sem=send, recv_sem=recv,
            device_id={"dp": where}, device_id_type=MESH,
        )

    def spread(self, group):
        for number, to in enumerate(self.peers):
            yield self.remote(
                self.slot.at[group, to], self.gathered[group].at[self.me],
                self.spread_send.at[group, number], self.spread_recv.at[group, number], to,
            )
        yield pltpu.make_async_copy(
            self.slot.at[group, self.me], self.gathered[group].at[self.me], self.local.at[group]
        )

    def spread_start(self, group):
        for copy in self.spread(group):
            copy.start()

    def spread_wait(self, group):
        for copy in self.spread(group):
            copy.wait()
        for number in range(group + 1):
            self.mine[PIECES[group] + number] = self.gathered[group][self.owner[0, number]]

    def pieces(self, group):
        return slice(PIECES[group], PIECES[group + 1])

    def keep_own(self, group):
        return pltpu.make_async_copy(
            self.mine.at[self.pieces(group)], self.factor.at[self.pieces(group), self.me],
            self.local.at[PANELS + group],
        )

    def send(self, group, role, who, rows, cols, where, source=None):
        at = (self.pieces(group), who, pl.ds(*rows), pl.ds(*cols))
        source = self.factor.at[at] if source is None else source
        number = len(self.started[group])
        self.remote(
            source, self.factor.at[at], self.pass_send.at[group, number],
            self.pass_recv.at[group, ROLES.index(role)], where,
        ).start()
        self.started[group].append((rows, cols))

    def wait(self, group, sem, rows, cols):
        view = self.factor.at[self.pieces(group), self.me, pl.ds(*rows), pl.ds(*cols)]
        pltpu.make_async_copy(view, view, sem).wait()

    def recv(self, group, role, rows=ALL, cols=FULL):
        self.wait(group, self.pass_recv.at[group, ROLES.index(role)], rows, cols)

    def stage_0(self, group):
        own = self.mine.at[self.pieces(group)]
        for role, where in (("z", self.z_peer), ("left", self.right), ("right", self.left), ("core0", self.other)):
            self.send(group, role, self.me, ALL, FULL, where, own)
        self.keep_own(group).start()

    def stage_1(self, group):
        self.recv(group, "z")
        self.send(group, "z_left_z", self.z_peer, Z_PART, FULL, self.right)
        self.send(group, "z_right_z", self.z_peer, Z_PART, FULL, self.left)
        self.send(group, "core1", self.z_peer, ALL, FULL, self.other)
        self.recv(group, "left")
        self.send(group, "far_lo", self.left, ALL, LOW, self.right)
        self.send(group, "z_left_x", self.left, X_PART, FULL, self.z_peer)
        self.send(group, "core2", self.left, ALL, FULL, self.other)
        self.recv(group, "right")
        self.send(group, "far_hi", self.right, ALL, HIGH, self.left)
        self.send(group, "z_right_x", self.right, X_PART, FULL, self.z_peer)
        self.send(group, "core3", self.right, ALL, FULL, self.other)

    def stage_2(self, group):
        self.recv(group, "far_lo", ALL, LOW)
        self.recv(group, "far_hi", ALL, HIGH)
        self.send(group, "z_far_x", self.far, X_PART, FULL, self.z_peer)
        self.send(group, "core4", self.far, ALL, FULL, self.other)
        self.recv(group, "z_left_z", Z_PART)
        self.send(group, "z_far_lo", self.z_left, Z_PART, LOW, self.right)
        self.recv(group, "z_right_z", Z_PART)
        self.send(group, "z_far_hi", self.z_right, Z_PART, HIGH, self.left)
        self.recv(group, "z_left_x", X_PART)
        self.send(group, "core5", self.z_left, ALL, FULL, self.other)
        self.recv(group, "z_right_x", X_PART)
        self.send(group, "core6", self.z_right, ALL, FULL, self.other)

    def stage_3(self, group):
        self.recv(group, "z_far_lo", Z_PART, LOW)
        self.recv(group, "z_far_hi", Z_PART, HIGH)
        self.recv(group, "z_far_x", X_PART)
        self.send(group, "core7", self.z_far, ALL, FULL, self.other)

    def arrived(self, group):
        for number in range(8):
            self.recv(group, "core%d" % number)
        self.keep_own(group).wait()

    def drain(self):
        for group in range(PANELS):
            for number, (rows, cols) in enumerate(self.started[group]):
                self.wait(group, self.pass_send.at[group, number], rows, cols)


def score_kernel(
    q_hbm, t_hbm, slot_hbm, owner_ref, count_ref, out_ref, factor,
    gather_0, gather_1, gather_2, gather_3, mine,
    l_high, l_low, x_ref, x_high, x_low, w_high, w_low, stage,
    a_in, b_in, tiles, first_in, second_out, second_in, kept, third_out, third_in,
    load_sem, stage_sem, a_send, a_recv, b_send, b_recv, r_send,
    f_send, f_recv, s_send, s_recv, m_send, m_recv, *pass_sems,
):
    me, section = lax.axis_index("dp"), lax.axis_index("section")
    count = lax.axis_size("dp")
    rings, row_of, half_of = 4, section // 2, section % 2
    even = me % 2 == 0
    odd = me % 2 == 1
    after, before_two = lax.rem(me + 1, count), lax.rem(me + count - 2, count)
    after_two = lax.rem(me + 2, count)
    exchange = Exchange(
        slot_hbm, owner_ref, factor, (gather_0, gather_1, gather_2, gather_3), mine, pass_sems
    )

    def section_at(steps):
        return lax.rem(row_of + steps, rings) * 2 + half_of

    partner = row_of * 2 + 1 - half_of
    barrier = pltpu.get_barrier_semaphore()
    for other in exchange.peers:
        pl.semaphore_signal(barrier, inc=1, device_id={"dp": other}, device_id_type=MESH)
    for other in (section_at(1), section_at(2), section_at(3), partner):
        pl.semaphore_signal(barrier, inc=1, device_id={"section": other}, device_id_type=MESH)

    copies = [
        pltpu.make_async_copy(source, x_ref.at[index], load_sem.at[index])
        for index, source in enumerate((q_hbm, t_hbm))
    ]
    for copy in copies:
        copy.start()
    pl.semaphore_wait(barrier, len(exchange.peers) + 4)
    exchange.spread_start(0)
    exchange.spread_start(1)
    for copy in copies:
        copy.wait()
    place = lax.broadcasted_iota(jnp.int32, (ROWS, SMALL), 0)
    keep = jnp.where(place < count_ref[0], F32(1.0 / 128.0), F32(0.0))
    for part in range(COORDS // SMALL):
        cols = slice(part * SMALL, (part + 1) * SMALL)
        x_ref[1, :, cols] = x_ref[1, :, cols] * keep

    def remote(source, target, send, recv, where):
        return pltpu.make_async_remote_copy(
            src_ref=source, dst_ref=target, send_sem=send, recv_sem=recv,
            device_id=where, device_id_type=MESH,
        )

    whole, early, last = pl.ds(0, ROWS), slice(0, COORDS - PANEL), pl.ds(COORDS - PANEL, PANEL)

    def chunk(part):
        return pl.ds(pl.multiple_of(part * CHUNK, CHUNK), CHUNK)

    def small_rows(part, base):
        return pl.ds(pl.multiple_of(base + part * PART, PART), PART)

    def group_cols(group):
        return pl.ds(group * PANEL, PANEL)

    def send_train(at, rows, cols):
        return remote(x_ref.at[1, rows, cols], a_in.at[rows, cols], a_send.at[at], a_recv.at[at], {"dp": after})

    def send_query(at, rows, cols):
        return remote(x_ref.at[0, rows, cols], b_in.at[rows, cols], b_send.at[at], b_recv.at[at], {"dp": before_two})

    def relay(at, rows, cols):
        return remote(a_in.at[rows, cols], b_in.at[rows, cols], r_send.at[at], b_recv.at[at], {"dp": after})

    def shift_group(group):
        send_train(group, whole, group_cols(group)).start()

        @pl.when(even)
        def _():
            send_query(group, whole, group_cols(group)).start()

    def relay_group(group):
        send_train(group, whole, group_cols(group)).wait_recv()

        @pl.when(even)
        def _():
            relay(group, whole, group_cols(group)).start()

    def load(group):
        load_group(group, factor, stage, stage_sem, l_high, l_low, w_high, w_low)

    def solve(group, half):
        solve_group(group, half, x_ref, x_high, x_low, l_high, l_low, w_high, w_low)

    def solve_both(group):
        @pl.loop(0, 2)
        def _(half):
            solve(group, half)

    for group in range(PANELS):
        exchange.spread_wait(group)
        exchange.stage_0(group)
        if group + 2 < PANELS:
            exchange.spread_start(group + 2)
        if group >= 1:
            exchange.stage_1(group - 1)
        if group >= 2:
            exchange.stage_2(group - 2)
        if group >= 3:
            exchange.stage_3(group - 3)
    exchange.arrived(0)
    load(0)
    solve_both(0)
    exchange.stage_1(3)
    exchange.stage_2(2)
    exchange.stage_3(1)
    shift_group(0)
    exchange.arrived(1)
    load(1)
    exchange.stage_2(3)
    exchange.stage_3(2)
    solve_both(1)
    exchange.stage_3(3)
    shift_group(1)
    exchange.arrived(2)
    load(2)
    solve_both(2)
    shift_group(2)
    exchange.arrived(3)
    load(3)

    @pl.loop(0, 2)
    def _(step):
        half = lax.rem(step + me, 2)
        solve(3, half)

        @pl.when(half == 1)
        def _():
            for part in range(4):
                send_train(3 + part, chunk(part), last).start()

        @pl.when((half == 0) & even)
        def _():
            for part in range(4):
                for piece in range(8):
                    send_query(3 + part, small_rows(part, piece * 64), last).start()

    def first_column(tile, part, steps):
        to = lax.rem(row_of + steps, rings)
        rows = pl.ds(pl.multiple_of(to * 128, 128), 128)
        at = tile * 4 + part
        return remote(
            tiles.at[tile, rows, chunk(part)], first_in.at[tile, steps - 1, :, chunk(part)],
            f_send.at[at, steps - 1], f_recv.at[at, steps - 1], {"section": section_at(steps)},
        )

    def first_row(part, steps, side):
        to = lax.rem(row_of + steps, rings)
        at = 8 + part
        return remote(
            tiles.at[2, small_rows(part, to * 128 + side * 64), :],
            first_in.at[2, steps - 1, small_rows(part, side * 64), :],
            f_send.at[at, steps - 1], f_recv.at[at, steps - 1], {"section": section_at(steps)},
        )

    def column_piece(tile, part, source):
        high, low = split(source[chunk(part), last])
        tiles[tile, :, chunk(part)] += dot3(x_high[0, :, last], x_low[0, :, last], high, low)
        for steps in (1, 2, 3):
            first_column(tile, part, steps).start()

    def keep_split(source, base):
        @pl.loop(0, ROWS // CHUNK)
        def _(part):
            high, low = split(source[chunk(part), early])
            there = pl.ds(pl.multiple_of(base + part * CHUNK, CHUNK), CHUNK)
            l_high[there, early] = high
            l_low[there, early] = low

    def first_waits(tile, part):
        for steps in (1, 2, 3):
            first_column(tile, part, steps).wait()

    def sum_columns(tile, part):
        first_waits(tile, part)
        for mine in (True, False):
            side = half_of if mine else 1 - half_of
            there = pl.ds(pl.multiple_of(side * 64, 64), 64)
            rows = pl.ds(pl.multiple_of(row_of * 128 + side * 64, 64), 64)
            total = tiles[tile, rows, chunk(part)]
            for steps in range(3):
                total = total + first_in[tile, steps, there, chunk(part)]
            if mine:
                kept[tile, :, chunk(part)] = total
            else:
                second_out[tile, :, chunk(part)] = total
        second_column(tile, part).start()

    def second_column(tile, part):
        at = tile * 4 + part
        return remote(
            second_out.at[tile, :, chunk(part)], second_in.at[tile, :, chunk(part)],
            s_send.at[at], s_recv.at[at], {"section": partner},
        )

    def end_columns(tile, part):
        second_column(tile, part).wait()
        there = pl.ds(pl.multiple_of(tile * ROWS + part * CHUNK, CHUNK), CHUNK)
        out_ref[:, there] = kept[tile, :, chunk(part)] + second_in[tile, :, chunk(part)]

    def sum_rows(part):
        first_waits(2, part)
        for mine in (True, False):
            side = half_of if mine else 1 - half_of
            total = tiles[2, small_rows(part, row_of * 128 + side * 64), :]
            for steps in range(3):
                total = total + first_in[2, steps, small_rows(part, side * 64), :]
            if mine:
                kept[2, small_rows(part, 0), :] = total
            else:
                second_out[2, small_rows(part, 0), :] = total
        second_row(part).start()

    def second_row(part):
        at = 8 + part
        return remote(
            second_out.at[2, small_rows(part, 0), :], second_in.at[2, small_rows(part, 0), :],
            s_send.at[at], s_recv.at[at], {"section": partner},
        )

    def move(part):
        return remote(
            third_out.at[small_rows(part, 0), :], third_in.at[small_rows(part, 0), :],
            m_send.at[part], m_recv.at[part], {"dp": after_two},
        )

    def end_rows(part):
        second_row(part).wait()
        rows = small_rows(part, 0)
        third_out[rows, :] = kept[2, rows, :] + second_in[2, rows, :]
        move(part).start()

    relay_group(0)
    relay_group(1)
    tiles[0] = dot3(x_high[0], x_low[0], x_high[1], x_low[1])
    for part in range(4):
        for steps in (1, 2, 3):
            first_column(0, part, steps).start()
    relay_group(2)
    keep_split(a_in, 0)
    tiles[1] = dot3(x_high[0, :, early], x_low[0, :, early], l_high[:ROWS, early], l_low[:ROWS, early])
    for group in range(PANELS - 1):
        view = b_in.at[whole, group_cols(group)]
        pltpu.make_async_copy(view, view, b_recv.at[group]).wait()
    keep_split(b_in, ROWS)
    second = slice(ROWS, 2 * ROWS)

    @pl.when(odd)
    def _():
        tiles[2] = dot3(x_high[0, :, early], x_low[0, :, early], l_high[second, early], l_low[second, early])

    @pl.when(even)
    def _():
        tiles[2] = dot3(l_high[second, early], l_low[second, early], x_high[1, :, early], x_low[1, :, early])

    @pl.loop(0, 7)
    def _(step):
        @pl.when(step < 4)
        def _():
            send_train(3 + step, chunk(step), last).wait()

            @pl.when(even)
            def _():
                relay(3 + step, chunk(step), last).start()

            column_piece(1, step, a_in)
            view = b_in.at[chunk(step), last]
            pltpu.make_async_copy(view, view, b_recv.at[3 + step]).wait()

            @pl.when(odd)
            def _():
                column_piece(2, step, b_in)

            @pl.when(even)
            def _():
                rows = [b_in[small_rows(step, piece * 64), last] for piece in range(8)]
                high, low = split(jnp.concatenate(rows, axis=0))
                made = dot3(high, low, x_high[1, :, last], x_low[1, :, last])
                for piece in range(8):
                    tiles[2, small_rows(step, piece * 64), :] += made[piece * PART : (piece + 1) * PART]
                for steps in (1, 2, 3):
                    for side in range(2):
                        first_row(step, steps, side).start()

            sum_columns(0, step)

        @pl.when((step >= 1) & (step < 5))
        def _():
            sum_columns(1, step - 1)

            @pl.when(odd)
            def _():
                sum_columns(2, step - 1)

            @pl.when(even)
            def _():
                sum_rows(step - 1)

            end_columns(0, step - 1)

        @pl.when((step >= 2) & (step < 6))
        def _():
            end_columns(1, step - 2)

            @pl.when(odd)
            def _():
                end_columns(2, step - 2)

            @pl.when(even)
            def _():
                end_rows(step - 2)

        @pl.when((step >= 3) & even)
        def _():
            move(step - 3).wait()
            out_ref[small_rows(step - 3, 0), 2 * ROWS :] = third_in[small_rows(step - 3, 0), :]

    @pl.when(even)
    def _():
        for group in range(PANELS - 1):
            relay(group, whole, group_cols(group)).wait_send()
            send_query(group, whole, group_cols(group)).wait_send()
        for part in range(4):
            relay(3 + part, chunk(part), last).wait_send()
            view = b_in.at[chunk(part), last]
            pltpu.make_async_copy(view, view, b_send.at[3 + part]).wait()

    for group in range(PANELS - 1):
        send_train(group, whole, group_cols(group)).wait_send()

    exchange.drain()


def scores_of(query, train, slot, owner, count):
    vmem, anyspace = pl.BlockSpec(memory_space=pltpu.VMEM), pl.BlockSpec(memory_space=pl.ANY)
    smem = pl.BlockSpec(memory_space=pltpu.SMEM)
    dma = pltpu.SemaphoreType.DMA
    scores, _ = pl.pallas_call(
        score_kernel,
        out_shape=(
            jax.ShapeDtypeStruct((64, 3 * ROWS), F32),
            jax.ShapeDtypeStruct((PIECES[-1], PEERS, STRIP, PANEL), F32),
        ),
        in_specs=[anyspace] * 3 + [smem] * 2,
        out_specs=(vmem, anyspace),
        scratch_shapes=[pltpu.VMEM((PEERS, STRIP, PANEL), F32)] * PANELS
        + [
            pltpu.VMEM((PIECES[-1], STRIP, PANEL), F32),
            pltpu.VMEM((COORDS, COORDS), BF16),
            pltpu.VMEM((COORDS, COORDS), BF16),
            pltpu.VMEM((2, ROWS, COORDS), F32),
            pltpu.VMEM((2, ROWS, COORDS), BF16),
            pltpu.VMEM((2, ROWS, COORDS), BF16),
            pltpu.VMEM((COORDS, BLOCK), BF16),
            pltpu.VMEM((COORDS, BLOCK), BF16),
            pltpu.VMEM((2, PEERS, STRIP, PANEL), F32),
            pltpu.VMEM((ROWS, COORDS), F32),
            pltpu.VMEM((ROWS, COORDS), F32),
            pltpu.VMEM((3, ROWS, ROWS), F32),
            pltpu.VMEM((3, 3, 128, ROWS), F32),
            pltpu.VMEM((3, 64, ROWS), F32),
            pltpu.VMEM((3, 64, ROWS), F32),
            pltpu.VMEM((3, 64, ROWS), F32),
            pltpu.VMEM((64, ROWS), F32),
            pltpu.VMEM((64, ROWS), F32),
            dma((2,)), dma((2,)), dma((7,)), dma((7,)), dma((7,)), dma((7,)), dma((7,)),
            dma((12, 3)), dma((12, 3)), dma((12,)), dma((12,)), dma((4,)), dma((4,)),
            dma((PANELS, PEERS - 1)), dma((PANELS, PEERS - 1)), dma((2 * PANELS,)),
            dma((PANELS, SENDS)), dma((PANELS, len(ROLES))),
        ],
        compiler_params=pltpu.CompilerParams(
            vmem_limit_bytes=63 << 20, collective_id=0, has_side_effects=True
        ),
        name="scores",
    )(query, train, slot, owner, count)
    return scores


def body(query_gradient_stack, train_grads, factor_slots, owner, train_count):
    slot = factor_slots.reshape(PANELS, PEERS, STRIP, PANEL)
    return scores_of(query_gradient_stack[0], train_grads[0], slot, owner, train_count)[None]


def solution(mesh):
    in_specs = (
        P("section", "dp", None),
        P("section", "dp", None),
        P("section", "dp", None, None),
        P("section", None),
        P("dp"),
    )
    out_specs = P("dp", "section", None)
    return jax.shard_map(body, mesh=mesh, in_specs=in_specs, out_specs=out_specs, check_vma=False)
```

```python
import jax
import jax.numpy as jnp
from jax import lax
from jax.experimental import pallas as pl
from jax.experimental.pallas import tpu as pltpu
from jax.sharding import PartitionSpec as P

COORDS = 2048
PANEL = 512
ROWS = 512
BLOCK = 256
SMALL = 128
BASE = 16
F32, BF16 = jnp.float32, jnp.bfloat16
NT = (((1,), (1,)), ((), ()))
NN = (((1,), (0,)), ((), ()))
MESH = pl.DeviceIdType.MESH
PANELS = COORDS // PANEL
CHUNK = 128
PART = 16
PEERS = 16
STRIP = PANEL // PEERS
Z_ROWS = STRIP // 2
EARLY = 2
PIECES = [group * (group + 1) // 2 for group in range(PANELS + 1)]


def split(value):
    high = value.astype(BF16)
    return high, (value - high.astype(F32)).astype(BF16)


def dot3(a_high, a_low, b_high, b_low, dims=NT):
    def one(a, b):
        return lax.dot_general(a, b, dims, preferred_element_type=F32)

    return one(a_high, b_high) + (one(a_high, b_low) + one(a_low, b_high))


def invert_small(blocks):
    row = lax.broadcasted_iota(jnp.int32, (SMALL, SMALL), 0)
    col = lax.broadcasted_iota(jnp.int32, (SMALL, SMALL), 1)
    groups = (SMALL // BASE, BASE)

    def substituted(block):
        diagonal = jnp.sum(jnp.where(row == col, block, 0.0), axis=1, keepdims=True)
        scale = (1.0 / diagonal).reshape(*groups, 1)
        inner = jnp.where(row // BASE == col // BASE, block, 0.0)
        inverse = jnp.where(row == col, 1.0, 0.0).reshape(*groups, SMALL)
        place = lax.broadcasted_iota(jnp.int32, inverse.shape, 1)
        for step in range(BASE):
            factor = jnp.sum(jnp.where(col % BASE == step, inner, 0.0), axis=1, keepdims=True)
            factor = jnp.where(place > step, factor.reshape(*groups, 1), 0.0)
            pivot = inverse[:, step : step + 1, :] * scale[:, step : step + 1, :]
            inverse = jnp.where(place == step, pivot, inverse - factor * pivot)
        return inverse.reshape(SMALL, SMALL)

    inverses = [substituted(block) for block in blocks]
    size = BASE
    while size < SMALL:
        pick = ((row // size) % 2 == 1) & (col // size == row // size - 1)
        halves = [split(inverse) for inverse in inverses]
        inner = [
            split(dot3(*split(jnp.where(pick, block, 0.0)), high, low, NN))
            for block, (high, low) in zip(blocks, halves)
        ]
        inverses = [
            inverse - dot3(*half, *middle, NN)
            for inverse, half, middle in zip(inverses, halves, inner)
        ]
        size *= 2
    return inverses


def load_group(group, factor, stage, stage_sem, l_high, l_low, w_high, w_low):
    def fetch(number):
        slot = number % 2
        return pltpu.make_async_copy(factor.at[PIECES[group] + number], stage.at[slot], stage_sem.at[slot])

    def strips(slot, first, rows, cols):
        part = stage[slot, first // STRIP : (first + rows) // STRIP, :, cols]
        return part.reshape(rows, part.shape[-1])

    fetch(0).start()
    for number in range(group + 1):
        if number < group:
            fetch(number + 1).start()
        fetch(number).wait()
        cols = slice(number * PANEL, (number + 1) * PANEL)

        @pl.loop(0, PANEL // CHUNK)
        def _(step):
            part = stage[number % 2, pl.ds(step * (CHUNK // STRIP), CHUNK // STRIP)]
            high, low = split(part.reshape(CHUNK, PANEL))
            there = pl.ds(pl.multiple_of(group * PANEL + step * CHUNK, CHUNK), CHUNK)
            l_high[there, cols] = high
            l_low[there, cols] = low

    slot = group % 2
    inverses = invert_small(
        [strips(slot, at, SMALL, slice(at, at + SMALL)) for at in range(0, PANEL, SMALL)]
    )
    for part in range(PANEL // BLOCK):
        at = part * BLOCK
        upper, lower = inverses[2 * part], inverses[2 * part + 1]
        cross = strips(slot, at + SMALL, SMALL, slice(at, at + SMALL))
        corner = -dot3(*split(lower), *split(dot3(*split(cross), *split(upper), NN)), NN)
        base = group * PANEL + at
        blank = jnp.zeros((SMALL, SMALL), F32)
        for value, rows, cols in ((upper, 0, 0), (corner, SMALL, 0), (lower, SMALL, SMALL), (blank, 0, SMALL)):
            high, low = split(value)
            w_high[base + rows : base + rows + SMALL, cols : cols + SMALL] = high
            w_low[base + rows : base + rows + SMALL, cols : cols + SMALL] = low


def solve_group(group, half, x_ref, x_high, x_low, l_high, l_low, w_high, w_low):
    base = group * PANEL
    cols = slice(base, base + PANEL)
    pending = x_ref[half, :, cols]
    if group:
        pending = pending - dot3(
            x_high[half, :, :base], x_low[half, :, :base], l_high[cols, :base], l_low[cols, :base]
        )
    for number in range(PANEL // BLOCK):
        at = base + number * BLOCK
        here, known = slice(at, at + BLOCK), slice(base, at)
        part = pending[:, number * BLOCK : (number + 1) * BLOCK]
        if number:
            part = part - dot3(
                x_high[half, :, known], x_low[half, :, known], l_high[here, known], l_low[here, known]
            )
        high, low = split(part)
        solved = dot3(high, low, w_high[here, :], w_low[here, :])
        x_ref[half, :, here] = solved
        high, low = split(solved)
        x_high[half, :, here] = high
        x_low[half, :, here] = low


def device_at(z, x, core):
    return lax.rem(z, 2) * 8 + lax.rem(x, 4) * 2 + lax.rem(core, 2)


ROLES = (
    "z", "left", "right", "far_lo", "far_hi", "z_left_z", "z_right_z", "z_left_x", "z_right_x",
    "z_far_lo", "z_far_hi", "z_far_x",
) + tuple("core%d" % number for number in range(8))
SENDS = 24
ALL, Z_PART, X_PART = (0, STRIP), (0, Z_ROWS), (Z_ROWS, STRIP - Z_ROWS)
FULL, LOW, HIGH = (0, PANEL), (0, PANEL // 2), (PANEL // 2, PANEL // 2)


class Exchange:
    def __init__(self, slot, owner, factor, gathered, chosen, pair, mine, sems):
        self.chosen, self.pair = chosen, pair
        self.slot, self.owner, self.factor, self.gathered, self.mine = slot, owner, factor, gathered, mine
        self.spread_send, self.spread_recv, self.local, self.pass_send, self.pass_recv, self.pair_sems = sems
        me = self.me = lax.axis_index("dp")
        self.z, self.x, self.core = z, x, core = me // 8, (me // 2) % 4, me % 2
        order = ((1, 0), (0, 1), (1, 3), (0, 2), (1, 1), (0, 3), (1, 2), (0, 0))
        steps = [(dz, dx, dc) for dz, dx in order for dc in (0, 1) if dz or dx or dc]
        self.same_core = [number for number, step in enumerate(steps) if step[2] == 0]
        self.peers = [
            device_at(z + dz, x + dx, core + dc) for dz, dx in order for dc in (0, 1) if dz or dx or dc
        ]
        self.z_peer, self.other = device_at(z + 1, x, core), device_at(z, x, core + 1)
        self.right, self.left = device_at(z, x + 1, core), device_at(z, x + 3, core)
        self.far = device_at(z, x + 2, core)
        self.z_left, self.z_right = device_at(z + 1, x + 3, core), device_at(z + 1, x + 1, core)
        self.z_far = device_at(z + 1, x + 2, core)
        self.started = [[] for _ in range(PANELS)]

    def remote(self, source, target, send, recv, where):
        return pltpu.make_async_remote_copy(
            src_ref=source, dst_ref=target, send_sem=send, recv_sem=recv,
            device_id={"dp": where}, device_id_type=MESH,
        )

    def pair_send(self):
        return self.remote(
            self.slot.at[0, :, 1 - self.core], self.pair, self.pair_sems.at[0], self.pair_sems.at[1], self.other
        )

    def pair_own(self):
        return pltpu.make_async_copy(self.slot.at[0, :, self.core], self.chosen, self.pair_sems.at[2])

    def pair_start(self):
        self.pair_send().start()
        self.pair_own().start()

    def pair_pick(self):
        self.pair_send().wait()
        self.pair_own().wait()
        self.chosen[...] = jnp.where(self.owner[0, 0] == self.me, self.chosen[...], self.pair[...])

    def spread_first(self):
        chip = self.me // 2
        for number, to in enumerate(self.peers):
            if number in self.same_core:
                yield self.remote(
                    self.chosen.at[to // 2], self.gathered[0].at[chip],
                    self.spread_send.at[0, number], self.spread_recv.at[0, number], to,
                )
        yield pltpu.make_async_copy(self.chosen.at[chip], self.gathered[0].at[chip], self.local.at[0])

    def spread(self, group):
        if group == 0:
            yield from self.spread_first()
            return
        for number, to in enumerate(self.peers):
            yield self.remote(
                self.slot.at[group, to // 2, to % 2], self.gathered[group].at[self.me],
                self.spread_send.at[group, number], self.spread_recv.at[group, number], to,
            )
        yield pltpu.make_async_copy(
            self.slot.at[group, self.me // 2, self.core], self.gathered[group].at[self.me], self.local.at[group]
        )

    def spread_start(self, group):
        for copy in self.spread(group):
            copy.start()

    def spread_wait(self, group):
        for copy in self.spread(group):
            copy.wait()
        for number in range(group + 1):
            source = self.owner[0, number] if group else lax.div(self.owner[0, number], 2)
            self.mine[PIECES[group] + number] = self.gathered[group][source]

    def pieces(self, group):
        return slice(PIECES[group], PIECES[group + 1])

    def keep_own(self, group):
        return pltpu.make_async_copy(
            self.mine.at[self.pieces(group)], self.factor.at[self.pieces(group), self.me],
            self.local.at[PANELS + group],
        )

    def send(self, group, role, who, rows, cols, where, source=None):
        at = (self.pieces(group), who, pl.ds(*rows), pl.ds(*cols))
        source = self.factor.at[at] if source is None else source
        number = len(self.started[group])
        self.remote(
            source, self.factor.at[at], self.pass_send.at[group, number],
            self.pass_recv.at[group, ROLES.index(role)], where,
        ).start()
        self.started[group].append((rows, cols))

    def wait(self, group, sem, rows, cols):
        view = self.factor.at[self.pieces(group), self.me, pl.ds(*rows), pl.ds(*cols)]
        pltpu.make_async_copy(view, view, sem).wait()

    def recv(self, group, role, rows=ALL, cols=FULL):
        self.wait(group, self.pass_recv.at[group, ROLES.index(role)], rows, cols)

    def stage_0(self, group):
        own = self.mine.at[self.pieces(group)]
        for role, where in (("z", self.z_peer), ("left", self.right), ("right", self.left), ("core0", self.other)):
            self.send(group, role, self.me, ALL, FULL, where, own)
        self.keep_own(group).start()

    def stage_1(self, group):
        self.recv(group, "z")
        self.send(group, "z_left_z", self.z_peer, Z_PART, FULL, self.right)
        self.send(group, "z_right_z", self.z_peer, Z_PART, FULL, self.left)
        self.send(group, "core1", self.z_peer, ALL, FULL, self.other)
        self.recv(group, "left")
        self.send(group, "far_lo", self.left, ALL, LOW, self.right)
        self.send(group, "z_left_x", self.left, X_PART, FULL, self.z_peer)
        self.send(group, "core2", self.left, ALL, FULL, self.other)
        self.recv(group, "right")
        self.send(group, "far_hi", self.right, ALL, HIGH, self.left)
        self.send(group, "z_right_x", self.right, X_PART, FULL, self.z_peer)
        self.send(group, "core3", self.right, ALL, FULL, self.other)

    def stage_2(self, group):
        self.recv(group, "far_lo", ALL, LOW)
        self.recv(group, "far_hi", ALL, HIGH)
        self.send(group, "z_far_x", self.far, X_PART, FULL, self.z_peer)
        self.send(group, "core4", self.far, ALL, FULL, self.other)
        self.recv(group, "z_left_z", Z_PART)
        self.send(group, "z_far_lo", self.z_left, Z_PART, LOW, self.right)
        self.recv(group, "z_right_z", Z_PART)
        self.send(group, "z_far_hi", self.z_right, Z_PART, HIGH, self.left)
        self.recv(group, "z_left_x", X_PART)
        self.send(group, "core5", self.z_left, ALL, FULL, self.other)
        self.recv(group, "z_right_x", X_PART)
        self.send(group, "core6", self.z_right, ALL, FULL, self.other)

    def stage_3(self, group):
        self.recv(group, "z_far_lo", Z_PART, LOW)
        self.recv(group, "z_far_hi", Z_PART, HIGH)
        self.recv(group, "z_far_x", X_PART)
        self.send(group, "core7", self.z_far, ALL, FULL, self.other)

    def arrived(self, group):
        for number in range(8):
            self.recv(group, "core%d" % number)
        self.keep_own(group).wait()

    def drain(self):
        for group in range(PANELS):
            for number, (rows, cols) in enumerate(self.started[group]):
                self.wait(group, self.pass_send.at[group, number], rows, cols)


def score_kernel(
    q_hbm, t_hbm, slot_hbm, owner_ref, count_ref, out_ref, factor,
    gather_0, gather_1, gather_2, gather_3, chosen, pair, mine,
    l_high, l_low, x_ref, x_high, x_low, w_high, w_low, stage,
    a_in, b_in, tiles, first_in, second_out, second_in, kept, third_in,
    load_sem, stage_sem, a_send, a_recv, b_send, b_recv, r_send,
    f_send, f_recv, s_send, s_recv, m_send, m_recv, *pass_sems,
):
    me, section = lax.axis_index("dp"), lax.axis_index("section")
    count = lax.axis_size("dp")
    rings, row_of, half_of = 4, section // 2, section % 2
    even = me % 2 == 0
    odd = me % 2 == 1
    after, before_two = lax.rem(me + 1, count), lax.rem(me + count - 2, count)
    after_two = lax.rem(me + 2, count)
    exchange = Exchange(
        slot_hbm, owner_ref, factor, (gather_0, gather_1, gather_2, gather_3), chosen, pair, mine, pass_sems
    )

    def section_at(steps):
        return lax.rem(row_of + steps, rings) * 2 + half_of

    partner = row_of * 2 + 1 - half_of
    barrier = pltpu.get_barrier_semaphore()
    for other in exchange.peers:
        pl.semaphore_signal(barrier, inc=1, device_id={"dp": other}, device_id_type=MESH)
    for other in (section_at(1), section_at(2), section_at(3), partner):
        pl.semaphore_signal(barrier, inc=1, device_id={"section": other}, device_id_type=MESH)
    pl.semaphore_signal(
        barrier, inc=1, device_id={"dp": before_two, "section": partner}, device_id_type=MESH
    )

    copies = [
        pltpu.make_async_copy(source, x_ref.at[index], load_sem.at[index])
        for index, source in enumerate((q_hbm, t_hbm))
    ]
    for copy in copies:
        copy.start()
    pl.semaphore_wait(barrier, len(exchange.peers) + 5)
    exchange.pair_start()
    exchange.spread_start(1)
    exchange.pair_pick()
    exchange.spread_start(0)
    exchange.spread_start(2)
    for copy in copies:
        copy.wait()
    place = lax.broadcasted_iota(jnp.int32, (ROWS, SMALL), 0)
    keep = jnp.where(place < count_ref[0], F32(1.0 / 128.0), F32(0.0))
    for part in range(COORDS // SMALL):
        cols = slice(part * SMALL, (part + 1) * SMALL)
        x_ref[1, :, cols] = x_ref[1, :, cols] * keep

    def remote(source, target, send, recv, where):
        return pltpu.make_async_remote_copy(
            src_ref=source, dst_ref=target, send_sem=send, recv_sem=recv,
            device_id=where, device_id_type=MESH,
        )

    whole, early = pl.ds(0, ROWS), slice(0, EARLY * PANEL)
    last = pl.ds(EARLY * PANEL, COORDS - EARLY * PANEL)

    def chunk(part):
        return pl.ds(pl.multiple_of(part * CHUNK, CHUNK), CHUNK)

    def small_rows(part, base):
        return pl.ds(pl.multiple_of(base + part * PART, PART), PART)

    def group_cols(group):
        return pl.ds(group * PANEL, PANEL)

    def send_train(at, rows, cols):
        return remote(x_ref.at[1, rows, cols], a_in.at[rows, cols], a_send.at[at], a_recv.at[at], {"dp": after})

    def send_query(at, rows, cols):
        return remote(x_ref.at[0, rows, cols], b_in.at[rows, cols], b_send.at[at], b_recv.at[at], {"dp": before_two})

    def relay(at, rows, cols):
        return remote(a_in.at[rows, cols], b_in.at[rows, cols], r_send.at[at], b_recv.at[at], {"dp": after})

    def shift_group(group):
        send_train(group, whole, group_cols(group)).start()

        @pl.when(even)
        def _():
            send_query(group, whole, group_cols(group)).start()

    def relay_group(group):
        send_train(group, whole, group_cols(group)).wait_recv()

        @pl.when(even)
        def _():
            relay(group, whole, group_cols(group)).start()

    def load(group):
        load_group(group, factor, stage, stage_sem, l_high, l_low, w_high, w_low)

    def solve(group, half):
        solve_group(group, half, x_ref, x_high, x_low, l_high, l_low, w_high, w_low)

    def solve_both(group):
        @pl.loop(0, 2)
        def _(half):
            solve(group, half)

    for group in range(PANELS):
        exchange.spread_wait(group)
        exchange.stage_0(group)
        if group == 0:
            exchange.spread_start(3)
        if group >= 1:
            exchange.stage_1(group - 1)
        if group >= 2:
            exchange.stage_2(group - 2)
        if group >= 3:
            exchange.stage_3(group - 3)
    exchange.arrived(0)
    load(0)
    solve_both(0)
    exchange.stage_1(3)
    exchange.stage_2(2)
    exchange.stage_3(1)
    exchange.arrived(1)
    load(1)
    exchange.stage_2(3)
    exchange.stage_3(2)
    solve_both(1)
    exchange.stage_3(3)
    shift_group(0)
    shift_group(1)
    exchange.arrived(2)
    load(2)
    solve_both(2)
    exchange.arrived(3)
    load(3)

    @pl.loop(0, 2)
    def _(step):
        half = lax.rem(step + me, 2)
        solve(3, half)

        @pl.when(half == 1)
        def _():
            for part in range(4):
                send_train(3 + part, chunk(part), last).start()

        @pl.when((half == 0) & even)
        def _():
            for part in range(4):
                for piece in range(8):
                    send_query(3 + part, small_rows(part, piece * 64), last).start()

    def first_column(tile, part, steps):
        to = lax.rem(row_of + steps, rings)
        rows = pl.ds(pl.multiple_of(to * 128, 128), 128)
        at = tile * 4 + part
        return remote(
            tiles.at[tile, rows, chunk(part)], first_in.at[tile, steps - 1, :, chunk(part)],
            f_send.at[at, steps - 1], f_recv.at[at, steps - 1], {"section": section_at(steps)},
        )

    def first_row(part, steps, side):
        to = lax.rem(row_of + steps, rings)
        at = 8 + part
        return remote(
            tiles.at[2, small_rows(part, to * 128 + side * 64), :],
            first_in.at[2, steps - 1, small_rows(part, side * 64), :],
            f_send.at[at, steps - 1], f_recv.at[at, steps - 1], {"section": section_at(steps)},
        )

    def column_piece(tile, part, source):
        high, low = split(source[chunk(part), last])
        tiles[tile, :, chunk(part)] += dot3(x_high[0, :, last], x_low[0, :, last], high, low)
        for steps in (1, 2, 3):
            first_column(tile, part, steps).start()

    def keep_split(source, base):
        @pl.loop(0, ROWS // CHUNK)
        def _(part):
            high, low = split(source[chunk(part), early])
            there = pl.ds(pl.multiple_of(base + part * CHUNK, CHUNK), CHUNK)
            l_high[there, early] = high
            l_low[there, early] = low

    def first_waits(tile, part):
        for steps in (1, 2, 3):
            first_column(tile, part, steps).wait()

    def sum_columns(tile, part):
        first_waits(tile, part)
        for mine in (True, False):
            side = half_of if mine else 1 - half_of
            there = pl.ds(pl.multiple_of(side * 64, 64), 64)
            rows = pl.ds(pl.multiple_of(row_of * 128 + side * 64, 64), 64)
            total = tiles[tile, rows, chunk(part)]
            for steps in range(3):
                total = total + first_in[tile, steps, there, chunk(part)]
            if mine:
                kept[tile, :, chunk(part)] = total
            else:
                second_out[tile, :, chunk(part)] = total
        second_column(tile, part).start()

    def second_column(tile, part):
        at = tile * 4 + part
        return remote(
            second_out.at[tile, :, chunk(part)], second_in.at[tile, :, chunk(part)],
            s_send.at[at], s_recv.at[at], {"section": partner},
        )

    def end_columns(tile, part):
        second_column(tile, part).wait()
        there = pl.ds(pl.multiple_of(tile * ROWS + part * CHUNK, CHUNK), CHUNK)
        out_ref[:, there] = kept[tile, :, chunk(part)] + second_in[tile, :, chunk(part)]

    def sum_rows(part):
        first_waits(2, part)
        for mine in (True, False):
            side = half_of if mine else 1 - half_of
            total = tiles[2, small_rows(part, row_of * 128 + side * 64), :]
            for steps in range(3):
                total = total + first_in[2, steps, small_rows(part, side * 64), :]
            if mine:
                kept[2, small_rows(part, 0), :] = total
            else:
                second_out[2, small_rows(part, 0), :] = total
        second_row(part).start()
        move(part).start()

    def second_row(part):
        at = 8 + part
        return remote(
            second_out.at[2, small_rows(part, 0), :], second_in.at[2, small_rows(part, 0), :],
            s_send.at[at], s_recv.at[at], {"dp": after_two, "section": partner},
        )

    def move(part):
        return remote(
            kept.at[2, small_rows(part, 0), :], third_in.at[small_rows(part, 0), :],
            m_send.at[part], m_recv.at[part], {"dp": after_two},
        )

    def end_rows(part):
        second_row(part).wait()
        move(part).wait()
        rows = small_rows(part, 0)
        out_ref[rows, 2 * ROWS :] = third_in[rows, :] + second_in[2, rows, :]

    for group in range(EARLY):
        relay_group(group)
    tiles[0] = dot3(x_high[0], x_low[0], x_high[1], x_low[1])
    for part in range(4):
        for steps in (1, 2, 3):
            first_column(0, part, steps).start()
    keep_split(a_in, 0)
    tiles[1] = dot3(x_high[0, :, early], x_low[0, :, early], l_high[:ROWS, early], l_low[:ROWS, early])
    for group in range(EARLY):
        view = b_in.at[whole, group_cols(group)]
        pltpu.make_async_copy(view, view, b_recv.at[group]).wait()
    keep_split(b_in, ROWS)
    second = slice(ROWS, 2 * ROWS)

    @pl.when(odd)
    def _():
        tiles[2] = dot3(x_high[0, :, early], x_low[0, :, early], l_high[second, early], l_low[second, early])

    @pl.when(even)
    def _():
        tiles[2] = dot3(l_high[second, early], l_low[second, early], x_high[1, :, early], x_low[1, :, early])

    @pl.when(odd)
    def _():
        @pl.loop(0, 4)
        def _(part):
            send_train(3 + part, chunk(part), last).wait()
            column_piece(1, part, a_in)

    @pl.loop(0, 6)
    def _(step):
        @pl.when(step < 4)
        def _():
            @pl.when(even)
            def _():
                send_train(3 + step, chunk(step), last).wait()
                relay(3 + step, chunk(step), last).start()
                column_piece(1, step, a_in)

            view = b_in.at[chunk(step), last]
            pltpu.make_async_copy(view, view, b_recv.at[3 + step]).wait()

            @pl.when(odd)
            def _():
                column_piece(2, step, b_in)

            @pl.when(even)
            def _():
                rows = [b_in[small_rows(step, piece * 64), last] for piece in range(8)]
                high, low = split(jnp.concatenate(rows, axis=0))
                made = dot3(high, low, x_high[1, :, last], x_low[1, :, last])
                for piece in range(8):
                    tiles[2, small_rows(step, piece * 64), :] += made[piece * PART : (piece + 1) * PART]
                for steps in (1, 2, 3):
                    for side in range(2):
                        first_row(step, steps, side).start()

            sum_columns(0, step)

        @pl.when((step >= 1) & (step < 5))
        def _():
            sum_columns(1, step - 1)

            @pl.when(odd)
            def _():
                sum_columns(2, step - 1)

            @pl.when(even)
            def _():
                sum_rows(step - 1)

            end_columns(0, step - 1)

        @pl.when((step >= 2) & (step < 6))
        def _():
            end_columns(1, step - 2)

            @pl.when(odd)
            def _():
                end_columns(2, step - 2)

            @pl.when(even)
            def _():
                end_rows(step - 2)

    @pl.when(even)
    def _():
        for group in range(EARLY):
            relay(group, whole, group_cols(group)).wait_send()
            send_query(group, whole, group_cols(group)).wait_send()
        for part in range(4):
            relay(3 + part, chunk(part), last).wait_send()
            view = b_in.at[chunk(part), last]
            pltpu.make_async_copy(view, view, b_send.at[3 + part]).wait()

    for group in range(EARLY):
        send_train(group, whole, group_cols(group)).wait_send()

    exchange.drain()


def scores_of(query, train, slot, owner, count):
    vmem, anyspace = pl.BlockSpec(memory_space=pltpu.VMEM), pl.BlockSpec(memory_space=pl.ANY)
    smem = pl.BlockSpec(memory_space=pltpu.SMEM)
    dma = pltpu.SemaphoreType.DMA
    scores, _ = pl.pallas_call(
        score_kernel,
        out_shape=(
            jax.ShapeDtypeStruct((64, 3 * ROWS), F32),
            jax.ShapeDtypeStruct((PIECES[-1], PEERS, STRIP, PANEL), F32),
        ),
        in_specs=[anyspace] * 3 + [smem] * 2,
        out_specs=(vmem, anyspace),
        scratch_shapes=[pltpu.VMEM((PEERS // 2, STRIP, PANEL), F32)]
        + [pltpu.VMEM((PEERS, STRIP, PANEL), F32)] * (PANELS - 1)
        + [
            pltpu.VMEM((PEERS // 2, STRIP, PANEL), F32),
            pltpu.VMEM((PEERS // 2, STRIP, PANEL), F32),
            pltpu.VMEM((PIECES[-1], STRIP, PANEL), F32),
            pltpu.VMEM((COORDS, COORDS), BF16),
            pltpu.VMEM((COORDS, COORDS), BF16),
            pltpu.VMEM((2, ROWS, COORDS), F32),
            pltpu.VMEM((2, ROWS, COORDS), BF16),
            pltpu.VMEM((2, ROWS, COORDS), BF16),
            pltpu.VMEM((COORDS, BLOCK), BF16),
            pltpu.VMEM((COORDS, BLOCK), BF16),
            pltpu.VMEM((2, PEERS, STRIP, PANEL), F32),
            pltpu.VMEM((ROWS, COORDS), F32),
            pltpu.VMEM((ROWS, COORDS), F32),
            pltpu.VMEM((3, ROWS, ROWS), F32),
            pltpu.VMEM((3, 3, 128, ROWS), F32),
            pltpu.VMEM((3, 64, ROWS), F32),
            pltpu.VMEM((3, 64, ROWS), F32),
            pltpu.VMEM((3, 64, ROWS), F32),
            pltpu.VMEM((64, ROWS), F32),
            dma((2,)), dma((2,)), dma((7,)), dma((7,)), dma((7,)), dma((7,)), dma((7,)),
            dma((12, 3)), dma((12, 3)), dma((12,)), dma((12,)), dma((4,)), dma((4,)),
            dma((PANELS, PEERS - 1)), dma((PANELS, PEERS - 1)), dma((2 * PANELS,)),
            dma((PANELS, SENDS)), dma((PANELS, len(ROLES))), dma((3,)),
        ],
        compiler_params=pltpu.CompilerParams(
            vmem_limit_bytes=63 << 20, collective_id=0, has_side_effects=True
        ),
        name="scores",
    )(query, train, slot, owner, count)
    return scores


def body(query_gradient_stack, train_grads, factor_slots, owner, train_count):
    slot = factor_slots.reshape(PANELS, PEERS // 2, 2, STRIP, PANEL)
    return scores_of(query_gradient_stack[0], train_grads[0], slot, owner, train_count)[None]


def solution(mesh):
    in_specs = (
        P("section", "dp", None),
        P("section", "dp", None),
        P("section", "dp", None, None),
        P("section", None),
        P("dp"),
    )
    out_specs = P("dp", "section", None)
    return jax.shard_map(body, mesh=mesh, in_specs=in_specs, out_specs=out_specs, check_vma=False)
```
